32 devices in a mesh: dp: 8 (over z, x), tensor: 4 (over y, core).
Axes of the slice: x: 2, y: 2, z: 4, core: 2. Of those that a mesh axis runs over, the one named last changes fastest.
Arguments:
- layer_input: bfloat16 [8192, 2048], P(('dp', 'tensor')), may hold values from -6 to 6
- segment_ids: int32 [8192], P('dp'), may hold values from 0 to 1023, as said below
- attn_gain: bfloat16 [2048], P('dp'), may hold values from 0.5 to 1.5
- query_weight: bfloat16 [2048, 2048], P('dp', 'tensor'), may hold values from -0.125 to 0.125
- key_weight: bfloat16 [2048, 512], P('dp', 'tensor'), may hold values from -0.125 to 0.125
- value_weight: bfloat16 [2048, 512], P('dp', 'tensor'), may hold values from -0.125 to 0.125
- output_weight: bfloat16 [2048, 2048], P('tensor', 'dp'), may hold values from -0.5 to 0.5
- mlp_gain: bfloat16 [2048], P('dp'), may hold values from 0.5 to 1.5
- gate_weight: bfloat16 [2048, 8192], P('dp', 'tensor'), may hold values from -0.125 to 0.125
- up_weight: bfloat16 [2048, 8192], P('dp', 'tensor'), may hold values from -0.125 to 0.125
- down_weight: bfloat16 [8192, 2048], P('tensor', 'dp'), may hold values from -0.0625 to 0.0625
- grad_output: bfloat16 [8192, 2048], P(('dp', 'tensor')), may hold values from -6 to 6
Outputs:
- layer_output: bfloat16 [8192, 2048], P(('dp', 'tensor'))
- grad_input: float32 [8192, 2048], P(('dp', 'tensor'))
- attn_gain_grad: float32 [2048], P('dp')
- query_weight_grad: float32 [2048, 2048], P('dp', 'tensor')
- key_weight_grad: float32 [2048, 512], P('dp', 'tensor')
- value_weight_grad: float32 [2048, 512], P('dp', 'tensor')
- output_weight_grad: float32 [2048, 2048], P('tensor', 'dp')
- mlp_gain_grad: float32 [2048], P('dp')
- gate_weight_grad: float32 [2048, 8192], P('dp', 'tensor')
- up_weight_grad: float32 [2048, 8192], P('dp', 'tensor')
- down_weight_grad: float32 [8192, 2048], P('tensor', 'dp')
The draws below stay inside these ranges and needn't reach their ends.
Inputs may be any that keep to these rules, and one draw needn't show every extreme that they name: `segment_ids`: within each aligned block of 1024 tokens (one index of dp) segment numbers start at 0 and never fall; every segment has 1 to 1024 tokens; some block holds segments of exactly 1024 tokens only, and some block holds segments of one token only.
All inputs are finite; a program needn't handle non-finite values.
Results may differ from the reference program's by a relative error of at most 0.02.
Values may be sent and summed in bfloat16 or wider, within the bound.
No kernel may reach another device: no remote copies, remote signals or barrier semaphores. Data moves between devices by JAX's collectives and lax.ppermute only.
A program may use at most 256 MiB of HBM per device.

```python
import jax
import jax.numpy as jnp
import numpy as np
from jax import lax

D = 2048
H = 32
KV = 8
HD = 64
FF = 8192
GROUP = 1024
SEQ_MAX = 1024
TOKENS = 8192
N_DP = 8


def draw_segment_ids(key, part):
    pick_key, level_key, cut_key = jax.random.split(key, 3)
    heaviest = jax.random.randint(pick_key, (), 0, N_DP)
    finest = (heaviest + 1) % N_DP
    periods = jnp.array([8, 32, 128, 512], dtype=jnp.int32)
    chosen = jax.random.randint(level_key, (N_DP,), 0, 4)
    period = jnp.sum(jnp.where(chosen[:, None] == jnp.arange(4, dtype=jnp.int32)[None, :], periods[None, :], 0), axis=1)
    random_bits = jax.random.randint(cut_key, (N_DP, GROUP), 0, 1048576)
    slot_index = jnp.arange(GROUP, dtype=jnp.int32)
    forced = slot_index % SEQ_MAX == 0
    random_cut = random_bits % period[:, None] == 0
    group_index = jnp.arange(N_DP, dtype=jnp.int32)
    boundary = forced[None, :] | random_cut & (group_index[:, None] != heaviest) | (group_index[:, None] == finest)
    numbers = jnp.cumsum(boundary.astype(jnp.int32), axis=1) - 1
    return numbers.reshape(N_DP * GROUP).astype(jnp.int32)


def level_of(own_key, extent, cuts, least, top_value):
    level = 1.0
    for axis_at, shards_of in cuts:
        draws = jax.random.uniform(jax.random.fold_in(jax.random.fold_in(own_key, 6), axis_at), (shards_of,), jnp.float32, least / len(cuts), top_value / len(cuts))
        level = level * jnp.repeat(jnp.exp(draws), extent[axis_at] // shards_of).reshape((-1,) + (1,) * (len(extent) - 1 - axis_at))
    return level


def scatter_about(rng, dims, spread, reach, shards=(), kind=jnp.bfloat16):
    values = spread * jax.random.normal(rng, dims, jnp.float32)
    if shards:
        values = values * level_of(rng, dims, shards, -0.22, 0.18)
    return jnp.clip(values, -reach, reach).astype(kind)


def setup_inputs(seed: int = 0) -> dict:
    streams_of = jax.random.split(jax.random.key(seed), 13)
    layer_input = scatter_about(streams_of[0], (TOKENS, D), 1.0, 6.0, ((0, 32),))
    segment_ids = draw_segment_ids(jax.random.fold_in(streams_of[12], 71), 0)
    attn_gain = jnp.clip(1.0 + 0.1 * jax.random.normal(streams_of[2], (D,), jnp.float32), 0.5, 1.5).astype(jnp.bfloat16)
    query_weight = scatter_about(streams_of[3], (D, H * HD), D ** -0.5, 0.125, ((0, 8), (1, 4)))
    key_weight = scatter_about(streams_of[4], (D, KV * HD), D ** -0.5, 0.125, ((0, 8), (1, 4)))
    value_weight = scatter_about(streams_of[5], (D, KV * HD), D ** -0.5, 0.125, ((0, 8), (1, 4)))
    output_weight = scatter_about(streams_of[6], (H * HD, D), (H * HD // 16) ** -0.5, 0.5, ((0, 4), (1, 8)))
    mlp_gain = jnp.clip(1.0 + 0.1 * jax.random.normal(streams_of[7], (D,), jnp.float32), 0.5, 1.5).astype(jnp.bfloat16)
    gate_weight = scatter_about(streams_of[8], (D, FF), D ** -0.5, 0.125, ((0, 8), (1, 4)))
    up_weight = scatter_about(streams_of[9], (D, FF), D ** -0.5, 0.125, ((0, 8), (1, 4)))
    down_weight = scatter_about(streams_of[10], (FF, D), FF ** -0.5, 0.0625, ((0, 4), (1, 8)))
    grad_output = scatter_about(streams_of[11], (TOKENS, D), 1.0, 6.0, ((0, 32),))
    return dict(layer_input=layer_input, segment_ids=segment_ids, attn_gain=attn_gain, query_weight=query_weight, key_weight=key_weight, value_weight=value_weight, output_weight=output_weight, mlp_gain=mlp_gain, gate_weight=gate_weight, up_weight=up_weight, down_weight=down_weight, grad_output=grad_output)


NORM_EPS = 1e-05
ROPE_BASE = 500000.0

@jax.custom_vjp
def low(v):
    return lax.optimization_barrier(v.astype(jnp.bfloat16)).astype(jnp.float32)

@jax.custom_vjp
def low_back(v):
    return v

def low_keep(v):
    return (low(v), None)

def low_pass(kept, grad):
    return (grad,)

def back_keep(v):
    return (v, None)

def back_low(kept, grad):
    return (low(grad),)
low.defvjp(low_keep, low_pass)
low_back.defvjp(back_keep, back_low)

def rope_frequencies(head_dim):
    base_freq = 1.0 / ROPE_BASE ** (np.arange(0, head_dim, 2) / head_dim)
    wavelen = 2.0 * np.pi / base_freq
    smooth = (8192.0 / wavelen - 1.0) / 3.0
    middle = (1.0 - smooth) * base_freq / 32.0 + smooth * base_freq
    return np.where(wavelen < 2048.0, base_freq, np.where(wavelen > 8192.0, base_freq / 32.0, middle))

def positions(segments):
    slot_index = jnp.arange(segments.shape[0], dtype=jnp.int32)
    starts_flag = jnp.concatenate([jnp.ones((1,), dtype=bool), segments[1:] != segments[:-1]])
    starts = lax.cummax(jnp.where(starts_flag, slot_index, 0), axis=0)
    return slot_index - starts

def rope_tables(segments, head_dim):
    offsets = positions(segments).astype(jnp.float32)
    frequencies = jnp.asarray(rope_frequencies(head_dim), dtype=jnp.float32)
    angles = offsets[:, None] * frequencies[None, :]
    angles = jnp.concatenate([angles, angles], axis=1)
    return (jnp.cos(angles), jnp.sin(angles))

def rotate(head_values, cosine_table, sine_table):
    half_width = head_values.shape[-1] // 2
    turned = jnp.concatenate([-head_values[..., half_width:], head_values[..., :half_width]], axis=-1)
    return head_values * cosine_table[:, None, :] + turned * sine_table[:, None, :]

def block_mask(segments, start, length):
    query_rows = start + jnp.arange(length, dtype=jnp.int32)
    query_segs = lax.dynamic_slice_in_dim(segments, start, length)
    key_rows = jnp.arange(segments.shape[0], dtype=jnp.int32)
    return (query_segs[:, None] == segments[None, :]) & (key_rows[None, :] <= query_rows[:, None])

def matmul_hi(left, right):
    return jnp.dot(left, right, precision=lax.Precision.HIGHEST, preferred_element_type=jnp.float32)

def rms_norm(rows_in, gain):
    scale_rows = lax.rsqrt(lax.optimization_barrier(jnp.mean(rows_in * rows_in, axis=-1, keepdims=True)) + NORM_EPS)
    return rows_in * scale_rows * gain

def attend_group(group_args):
    query_raw, key_raw, value_raw, segments = group_args
    cosine_table, sine_table = rope_tables(segments, HD)
    queries = low(rotate(low_back(query_raw), cosine_table, sine_table))
    rot_keys = low(rotate(low_back(key_raw), cosine_table, sine_table))
    value_rows = low(low_back(value_raw))
    grouped = queries.reshape(GROUP, KV, H // KV, HD)
    scores = jnp.einsum('qgrd,kgd->grqk', grouped, rot_keys, precision=lax.Precision.HIGHEST) * HD ** (-0.5)
    scores = low_back(scores)
    visible = block_mask(segments, 0, GROUP)
    masked_scores = jnp.where(visible, scores, 0.0)
    weights = jnp.where(visible, jnp.exp(masked_scores), 0.0)
    probability = low(weights / lax.optimization_barrier(jnp.sum(weights, axis=-1, keepdims=True)))
    attended = jnp.einsum('grqk,kgd->qgrd', probability, value_rows, precision=lax.Precision.HIGHEST)
    return low(low_back(attended.reshape(GROUP, H * HD)))

def forward(inputs, attn_gain, query_weight, key_weight, value_weight, output_weight, mlp_gain, gate_weight, up_weight, down_weight, segment_ids):
    attn_normed = low(rms_norm(inputs, attn_gain))
    query_raw = matmul_hi(attn_normed, query_weight).reshape(N_DP, GROUP, H, HD)
    key_raw = matmul_hi(attn_normed, key_weight).reshape(N_DP, GROUP, KV, HD)
    value_raw = matmul_hi(attn_normed, value_weight).reshape(N_DP, GROUP, KV, HD)
    group_segs = segment_ids.reshape(N_DP, GROUP)
    attended = lax.map(jax.checkpoint(attend_group), (query_raw, key_raw, value_raw, group_segs))
    attended = attended.reshape(N_DP * GROUP, H * HD)
    residual = inputs + low_back(matmul_hi(attended, output_weight))
    mlp_normed = low(rms_norm(residual, mlp_gain))
    gate_pre = low_back(matmul_hi(mlp_normed, gate_weight))
    up_pre = low_back(matmul_hi(mlp_normed, up_weight))
    hidden = low(jax.nn.silu(gate_pre) * up_pre)
    return residual + low_back(matmul_hi(hidden, down_weight))

def reference(layer_input, segment_ids, attn_gain, query_weight, key_weight, value_weight, output_weight, mlp_gain, gate_weight, up_weight, down_weight, grad_output):
    params = tuple((weight.astype(jnp.float32) for weight in (attn_gain, query_weight, key_weight, value_weight, output_weight, mlp_gain, gate_weight, up_weight, down_weight)))
    inputs = layer_input.astype(jnp.float32)

    def run_layer(layer_in, *weights):
        return forward(layer_in, *weights, segment_ids)
    result, pullback = jax.vjp(run_layer, inputs, *params)
    gradients = pullback(grad_output.astype(jnp.float32))
    return (result.astype(jnp.bfloat16), gradients[0], gradients[1], gradients[2], gradients[3], gradients[4], gradients[5], gradients[6], gradients[7], gradients[8], gradients[9])
```

```python
import functools

import jax
import jax.numpy as jnp
import numpy as np
from jax import lax
from jax.experimental import pallas as pl
from jax.experimental.pallas import tpu as pltpu
from jax.sharding import PartitionSpec as P

HD = 64
NORM_EPS = 1e-05
ROPE_BASE = 500000.0
F32 = jnp.float32
BF16 = jnp.bfloat16
LANES = 128


def rope_frequencies(head_dim):
    base_freq = 1.0 / ROPE_BASE ** (np.arange(0, head_dim, 2) / head_dim)
    wavelen = 2.0 * np.pi / base_freq
    smooth = (8192.0 / wavelen - 1.0) / 3.0
    middle = (1.0 - smooth) * base_freq / 32.0 + smooth * base_freq
    return np.where(
        wavelen < 2048.0, base_freq, np.where(wavelen > 8192.0, base_freq / 32.0, middle)
    )


def positions(segments):
    slot_index = jnp.arange(segments.shape[0], dtype=jnp.int32)
    starts_flag = jnp.concatenate([jnp.ones((1,), dtype=bool), segments[1:] != segments[:-1]])
    starts = lax.cummax(jnp.where(starts_flag, slot_index, 0), axis=0)
    return slot_index - starts


def rope_tables(segments):
    offsets = positions(segments).astype(F32)
    frequencies = jnp.asarray(rope_frequencies(HD), dtype=F32)
    angles = offsets[:, None] * frequencies[None, :]
    cosine, sine = jnp.cos(angles), jnp.sin(angles)
    return (
        jnp.concatenate([cosine] * 4, axis=1),
        jnp.concatenate([-sine, sine, -sine, sine], axis=1),
    )


def half_swap(v):
    lane = lax.broadcasted_iota(jnp.int32, v.shape, 1)
    return jnp.where(lane % HD < HD // 2, pltpu.roll(v, LANES - HD // 2, 1), pltpu.roll(v, HD // 2, 1))


def dot(a, b, ca, cb):
    return lax.dot_general(a, b, (((ca,), (cb,)), ((), ())), preferred_element_type=F32)


def full(shape):
    return pl.BlockSpec(shape, lambda *_: (0,) * len(shape))


def qkv_kernel(n_rot, x_ref, w_ref, cos_ref, sin_ref, out_ref):
    raw = jnp.dot(x_ref[...], w_ref[...], preferred_element_type=F32)
    cosine, sine = cos_ref[...], sin_ref[...]
    for at in range(0, raw.shape[1], LANES):
        part = raw[:, at : at + LANES]
        if at < n_rot:
            part = part * cosine + half_swap(part) * sine
        out_ref[:, at : at + LANES] = part.astype(BF16)


def qkv_project(rows, weight, cosine, sine, n_rot):
    tokens, width = rows.shape
    cols = weight.shape[1]
    tile = 256
    return pl.pallas_call(
        functools.partial(qkv_kernel, n_rot),
        grid=(tokens // tile,),
        in_specs=[
            pl.BlockSpec((tile, width), lambda i: (i, 0)),
            full((width, cols)),
            pl.BlockSpec((tile, LANES), lambda i: (i, 0)),
            pl.BlockSpec((tile, LANES), lambda i: (i, 0)),
        ],
        out_specs=pl.BlockSpec((tile, cols), lambda i: (i, 0)),
        out_shape=jax.ShapeDtypeStruct((tokens, cols), BF16),
        cost_estimate=pl.CostEstimate(
            flops=2 * tokens * width * cols,
            bytes_accessed=2 * (tokens * width + width * cols + tokens * cols),
            transcendentals=0,
        ),
        name="qkv_project",
    )(rows, weight, cosine, sine)


TILE = 256


def stacked(pair, scale=None):
    lane = lax.broadcasted_iota(jnp.int32, pair.shape, 1)
    if scale is not None:
        pair = pair * jnp.asarray(scale, pair.dtype)
    zero = jnp.zeros_like(pair)
    return jnp.concatenate(
        [jnp.where(lane < HD, pair, zero), jnp.where(lane >= HD, pair, zero)], axis=0
    )


def unstacked(both):
    lane = lax.broadcasted_iota(jnp.int32, (TILE, LANES), 1)
    return jnp.where(lane < HD, both[:TILE], both[TILE:])


def visible_pair(seg_col, seg_row, key_start, row_start):
    keys = key_start + lax.broadcasted_iota(jnp.int32, (TILE, TILE), 0)
    rows = row_start + lax.broadcasted_iota(jnp.int32, (TILE, TILE), 1)
    one = (seg_col == seg_row) & (keys <= rows)
    return jnp.concatenate([one, one], axis=1)


def attn_fwd_kernel(qkv_ref, k_ref, v_ref, segc_ref, segr_ref, out_ref, inv_ref, w_ref, vt_ref):
    tile = pl.program_id(0)

    @pl.when(tile == 0)
    def _():
        vt_ref[...] = v_ref[...].astype(F32).T.astype(BF16)

    row_start = tile * TILE
    seg_row = segr_ref[:, pl.ds(pl.multiple_of(row_start, TILE), TILE)]
    slices = out_ref.shape[1] // LANES
    for s in range(slices):
        q2 = stacked(qkv_ref[:, s * LANES : (s + 1) * LANES], HD**-0.5)

        def score(c, total):
            at = pl.multiple_of(c * TILE, TILE)
            sc = dot(k_ref[pl.ds(at, TILE), :], q2, 1, 1)
            seen = visible_pair(segc_ref[pl.ds(at, TILE), :], seg_row, at, row_start)
            w = jnp.where(seen, jnp.exp(jnp.where(seen, sc, 0.0)), 0.0)
            w_ref[pl.ds(at, TILE), :] = w
            return total + jnp.sum(w, axis=0, keepdims=True)

        total = lax.fori_loop(0, tile + 1, score, jnp.zeros((1, 2 * TILE), F32))
        inv = 1.0 / total
        inv_ref[0, s : s + 1, :] = inv

        def attend(c, acc):
            at = pl.multiple_of(c * TILE, TILE)
            p = (w_ref[pl.ds(at, TILE), :] * inv).astype(BF16)
            return acc + dot(vt_ref[:, pl.ds(at, TILE)], p, 1, 0)

        acc = lax.fori_loop(0, tile + 1, attend, jnp.zeros((LANES, 2 * TILE), F32))
        out_ref[:, s * LANES : (s + 1) * LANES] = unstacked(acc.T).astype(BF16)


def attend_forward(qkv, seg_col, seg_row, n_q):
    tokens = qkv.shape[0]
    slices = n_q // LANES
    tiles = tokens // TILE
    k_at, v_at = n_q // LANES, n_q // LANES + 1
    pairs = tokens * (tokens + TILE) // 2
    return pl.pallas_call(
        attn_fwd_kernel,
        grid=(tiles,),
        in_specs=[
            pl.BlockSpec((TILE, n_q), lambda i: (i, 0)),
            pl.BlockSpec((tokens, LANES), lambda i: (0, k_at)),
            pl.BlockSpec((tokens, LANES), lambda i: (0, v_at)),
            full((tokens, 1)),
            full((1, tokens)),
        ],
        out_specs=[
            pl.BlockSpec((TILE, n_q), lambda i: (i, 0)),
            pl.BlockSpec((1, slices, 2 * TILE), lambda i: (i, 0, 0)),
        ],
        out_shape=[
            jax.ShapeDtypeStruct((tokens, n_q), BF16),
            jax.ShapeDtypeStruct((tiles, slices, 2 * TILE), F32),
        ],
        scratch_shapes=[pltpu.VMEM((tokens, 2 * TILE), F32), pltpu.VMEM((LANES, tokens), BF16)],
        cost_estimate=pl.CostEstimate(
            flops=pairs * n_q * 2 * 16,
            bytes_accessed=2 * tokens * (2 * n_q + 4 * LANES),
            transcendentals=pairs * n_q // HD,
        ),
        name="attend_forward",
    )(qkv, qkv, qkv, seg_col, seg_row)


def attn_bwd_kernel(
    q_ref, k_ref, v_ref, do_ref, inv_ref, segc_ref, segr_ref, cos_ref, sin_ref, cosf_ref, sinf_ref,
    dq_ref, dkv_ref, p_ref, dp_ref, kt_ref, dk_acc, dv_acc,
):
    tile = pl.program_id(0)
    scale = HD**-0.5

    @pl.when(tile == 0)
    def _():
        kt_ref[...] = (k_ref[...].astype(F32).T * scale).astype(BF16)
        dk_acc[...] = jnp.zeros_like(dk_acc)
        dv_acc[...] = jnp.zeros_like(dv_acc)

    row_start = tile * TILE
    seg_row = segr_ref[:, pl.ds(pl.multiple_of(row_start, TILE), TILE)]
    slices = q_ref.shape[1] // LANES
    for s in range(slices):
        q2 = stacked(q_ref[:, s * LANES : (s + 1) * LANES], scale)
        do2 = stacked(do_ref[:, s * LANES : (s + 1) * LANES])
        inv = inv_ref[0, s : s + 1, :]

        def first(c, delta):
            at = pl.multiple_of(c * TILE, TILE)
            sc = dot(k_ref[pl.ds(at, TILE), :], q2, 1, 1)
            dp = dot(v_ref[pl.ds(at, TILE), :], do2, 1, 1)
            seen = visible_pair(segc_ref[pl.ds(at, TILE), :], seg_row, at, row_start)
            p = jnp.where(seen, jnp.exp(jnp.where(seen, sc, 0.0)) * inv, 0.0)
            p_ref[pl.ds(at, TILE), :] = p
            dp_ref[pl.ds(at, TILE), :] = dp
            return delta + jnp.sum(p * dp, axis=0, keepdims=True)

        delta = lax.fori_loop(0, tile + 1, first, jnp.zeros((1, 2 * TILE), F32))

        def second(c, dq):
            at = pl.multiple_of(c * TILE, TILE)
            p = p_ref[pl.ds(at, TILE), :]
            ds = (p * (dp_ref[pl.ds(at, TILE), :] - delta)).astype(BF16)
            dv_acc[pl.ds(at, TILE), :] += dot(p.astype(BF16), do2, 1, 0)
            dk_acc[pl.ds(at, TILE), :] += dot(ds, q2, 1, 0)
            return dq + dot(kt_ref[:, pl.ds(at, TILE)], ds, 1, 0)

        dq = lax.fori_loop(0, tile + 1, second, jnp.zeros((LANES, 2 * TILE), F32))
        dq = unstacked(dq.T)
        dq_ref[:, s * LANES : (s + 1) * LANES] = (
            dq * cos_ref[...] - half_swap(dq) * sin_ref[...]
        ).astype(BF16)

    @pl.when(tile == pl.num_programs(0) - 1)
    def _():
        dk = dk_acc[...]
        dkv_ref[:, :LANES] = (dk * cosf_ref[...] - half_swap(dk) * sinf_ref[...]).astype(BF16)
        dkv_ref[:, LANES:] = dv_acc[...].astype(BF16)


def attend_backward(qkv, grad_attended, inv, seg_col, seg_row, cosine, sine, n_q):
    tokens = qkv.shape[0]
    slices = n_q // LANES
    tiles = tokens // TILE
    k_at, v_at = n_q // LANES, n_q // LANES + 1
    pairs = tokens * (tokens + TILE) // 2
    return pl.pallas_call(
        attn_bwd_kernel,
        grid=(tiles,),
        in_specs=[
            pl.BlockSpec((TILE, n_q), lambda i: (i, 0)),
            pl.BlockSpec((tokens, LANES), lambda i: (0, k_at)),
            pl.BlockSpec((tokens, LANES), lambda i: (0, v_at)),
            pl.BlockSpec((TILE, n_q), lambda i: (i, 0)),
            pl.BlockSpec((1, slices, 2 * TILE), lambda i: (i, 0, 0)),
            full((tokens, 1)),
            full((1, tokens)),
            pl.BlockSpec((TILE, LANES), lambda i: (i, 0)),
            pl.BlockSpec((TILE, LANES), lambda i: (i, 0)),
            full((tokens, LANES)),
            full((tokens, LANES)),
        ],
        out_specs=[
            pl.BlockSpec((TILE, n_q), lambda i: (i, 0)),
            full((tokens, 2 * LANES)),
        ],
        out_shape=[
            jax.ShapeDtypeStruct((tokens, n_q), BF16),
            jax.ShapeDtypeStruct((tokens, 2 * LANES), BF16),
        ],
        scratch_shapes=[
            pltpu.VMEM((tokens, 2 * TILE), F32),
            pltpu.VMEM((tokens, 2 * TILE), F32),
            pltpu.VMEM((LANES, tokens), BF16),
            pltpu.VMEM((tokens, LANES), F32),
            pltpu.VMEM((tokens, LANES), F32),
        ],
        cost_estimate=pl.CostEstimate(
            flops=pairs * n_q * 5 * 16,
            bytes_accessed=2 * tokens * (3 * n_q + 8 * LANES),
            transcendentals=pairs * n_q // HD,
        ),
        name="attend_backward",
    )(qkv, qkv, qkv, grad_attended, inv, seg_col, seg_row, cosine, sine, cosine, sine)


def rms_forward(rows_in, gain):
    scale_rows = lax.rsqrt(jnp.mean(rows_in * rows_in, axis=-1, keepdims=True) + NORM_EPS)
    normed = rows_in * scale_rows
    return (normed, scale_rows, normed * gain)


def rms_backward(grad_out, normed, scale_rows, gain):
    scaled_grad = grad_out * gain
    grad_rows = scale_rows * (
        scaled_grad - normed * jnp.mean(scaled_grad * normed, axis=-1, keepdims=True)
    )
    return (grad_rows, jnp.sum(grad_out * normed, axis=0))


class Ranks:
    def __init__(self, n_dp, n_tensor):
        self.sizes = {"dp": n_dp, "tensor": n_tensor}
        self.dp = lax.axis_index("dp")
        self.tensor = lax.axis_index("tensor")
        self.lo = 2 if n_dp >= 4 else 0
        bits = [1 << b for b in reversed(range(n_dp.bit_length() - 1))]
        self.all_bits = bits
        self.mlp_bits = [b for b in bits if b != self.lo]
        self.side = (self.dp // 2) % 2 if self.lo else 0

    def swap(self, value, axis, bit):
        return lax.ppermute(value, axis, [(i, i ^ bit) for i in range(self.sizes[axis])])

    def gather(self, pieces, bits):
        pieces = dict(pieces)
        for bit in bits:
            for offset in list(pieces):
                pieces[offset ^ bit] = self.swap(pieces[offset], "dp", bit)
        return pieces

    def lay_out(self, pieces, axis):
        first = pieces[0]
        shape = list(first.shape)
        width = shape[axis]
        shape[axis] = width * len(pieces)
        whole = jnp.zeros(tuple(shape), first.dtype)
        for offset, piece in pieces.items():
            whole = lax.dynamic_update_slice_in_dim(whole, piece, (self.dp ^ offset) * width, axis)
        return whole

    def block(self, whole, offset, width, axis):
        return lax.dynamic_slice_in_dim(whole, (self.dp ^ offset) * width, width, axis)

    def reduce(self, terms, bits):
        terms = dict(terms)
        for bit in reversed(bits):
            sent = {}
            for offset in sorted((o for o in terms if o & bit), reverse=True):
                sent[offset ^ bit] = self.swap(terms.pop(offset).astype(BF16), "dp", bit)
            for offset, came in sent.items():
                terms[offset] = terms[offset].astype(F32) + came.astype(F32)
        return terms

    def halves(self, weight, axis):
        width = weight.shape[axis] // 2
        own = lax.dynamic_slice_in_dim(weight, self.side * width, width, axis)
        other = lax.dynamic_slice_in_dim(weight, (1 - self.side) * width, width, axis)
        return own, other

    def gather_split(self, weight, split_axis, lay_axis):
        own, other = self.halves(weight, split_axis)
        pieces = {0: own, self.lo: self.swap(other, "dp", self.lo)}
        return self.lay_out(self.gather(pieces, self.mlp_bits), lay_axis)

    def reduce_split(self, whole, split_axis, lay_axis, width):
        terms = {
            offset: self.block(whole, offset, width, lay_axis)
            for offset in range(self.sizes["dp"])
        }
        terms = self.reduce(terms, self.mlp_bits)
        own = terms[0].astype(F32)
        came = self.swap(terms[self.lo].astype(BF16), "dp", self.lo).astype(F32)
        first = jnp.where(self.side == 0, own, came)
        last = jnp.where(self.side == 0, came, own)
        return jnp.concatenate([first, last], axis=split_axis)

    def gather_group(self, rows):
        near = self.swap(rows, "tensor", 1)
        far = self.swap(rows, "tensor", 2)
        pieces = {0: rows, 1: near, 2: far, 3: self.swap(far, "tensor", 1)}
        count = rows.shape[0]
        whole = jnp.zeros((count * 4, rows.shape[1]), rows.dtype)
        for offset, piece in pieces.items():
            whole = lax.dynamic_update_slice_in_dim(whole, piece, (self.tensor ^ offset) * count, 0)
        return whole

    def scatter_group(self, terms):
        count = terms.shape[0] // 4

        def part(offset):
            return lax.dynamic_slice_in_dim(terms, (self.tensor ^ offset) * count, count, 0)

        far = part(2).astype(F32) + self.swap(part(3), "tensor", 1).astype(F32)
        near = part(0).astype(F32) + self.swap(part(1), "tensor", 1).astype(F32)
        return near + self.swap(far.astype(BF16), "tensor", 2).astype(F32)

    def gather_pair(self, rows):
        half = rows.shape[0] // 2
        far = self.swap(rows, "tensor", 2)
        side = self.swap(rows, "dp", self.lo)
        near = self.swap(rows, "tensor", 1)
        top = self.swap(side[:half], "tensor", 2)
        bottom = self.swap(far[half:], "dp", self.lo)
        own = [rows, far, side, top, bottom]
        across = [near] + [self.swap(piece, "tensor", 1) for piece in own[1:]]
        return jnp.concatenate(own + across, axis=0)

    def scatter_pair(self, terms):
        count = terms.shape[0] // 8
        half = count // 2
        mine, theirs = terms[: 4 * count], terms[4 * count :]

        def met(offset, rows):
            lo = offset * count
            return mine[lo : lo + rows].astype(F32) + self.swap(
                theirs[lo : lo + rows], "tensor", 1
            ).astype(F32)

        corner = met(3, count)
        far, side, own = met(1, count), met(2, count), met(0, count)
        top = self.swap(corner[:half].astype(BF16), "tensor", 2).astype(F32)
        bottom = self.swap(corner[half:].astype(BF16), "dp", self.lo).astype(F32)
        side = jnp.concatenate([side[:half] + top, side[half:]], axis=0).astype(BF16)
        far = jnp.concatenate([far[:half], far[half:] + bottom], axis=0).astype(BF16)
        return own + self.swap(far, "tensor", 2).astype(F32) + self.swap(side, "dp", self.lo).astype(F32)

    def sum_everywhere(self, value):
        for axis in ("tensor", "dp"):
            bit = 1
            while bit < self.sizes[axis]:
                value = value + self.swap(value, axis, bit)
                bit *= 2
        return value


def paired_heads(weight, axis, repeat):
    shape = weight.shape
    heads = shape[axis] // HD
    split = shape[:axis] + (heads // repeat, repeat, HD) + shape[axis + 1 :]
    return jnp.swapaxes(weight.reshape(split), axis, axis + 1).reshape(shape)


def unpaired_heads(weight, axis, repeat):
    shape = weight.shape
    heads = shape[axis] // HD
    split = shape[:axis] + (repeat, heads // repeat, HD) + shape[axis + 1 :]
    return jnp.swapaxes(weight.reshape(split), axis, axis + 1).reshape(shape)


def per_device(
    n_dp,
    n_tensor,
    layer_input,
    segment_ids,
    attn_gain,
    query_weight,
    key_weight,
    value_weight,
    output_weight,
    mlp_gain,
    gate_weight,
    up_weight,
    down_weight,
    grad_output,
):
    ranks = Ranks(n_dp, n_tensor)
    width = layer_input.shape[1]
    shard = query_weight.shape[0]
    n_q, n_kv = query_weight.shape[1], key_weight.shape[1]
    repeat = n_q // n_kv
    gains = ranks.gather({0: jnp.stack([attn_gain, mlp_gain])}, ranks.all_bits)
    qkv_own = jnp.concatenate(
        [paired_heads(query_weight, 1, repeat), key_weight, value_weight], axis=1
    )
    qkv_weight = ranks.lay_out(ranks.gather({0: qkv_own}, ranks.all_bits), 0)
    out_weight = ranks.lay_out(
        ranks.gather({0: paired_heads(output_weight, 0, repeat)}, ranks.all_bits), 1
    )
    gains = ranks.lay_out(gains, 1).astype(F32)
    attn_g, mlp_g = gains[0], gains[1]
    gate_full = ranks.gather_split(gate_weight, 1, 0)
    up_full = ranks.gather_split(up_weight, 1, 0)
    down_full = ranks.gather_split(down_weight, 0, 1)

    inputs = layer_input.astype(F32)
    attn_normed, attn_scale, attn_out = rms_forward(inputs, attn_g)
    attn_rows = ranks.gather_group(attn_out.astype(BF16))
    cosine, sine = rope_tables(segment_ids)
    seg_col, seg_row = segment_ids[:, None], segment_ids[None, :]
    qkv = qkv_project(attn_rows, qkv_weight, cosine, sine, n_q + n_kv)
    attended, inv = attend_forward(qkv, seg_col, seg_row, n_q)
    attn_terms = jnp.dot(attended, out_weight, preferred_element_type=F32).astype(BF16)
    residual = inputs + ranks.scatter_group(attn_terms)
    mlp_normed, mlp_scale, mlp_out = rms_forward(residual, mlp_g)
    mlp_rows = ranks.gather_pair(mlp_out.astype(BF16))
    grad_rows = ranks.gather_pair(grad_output)
    gate_pre = jnp.dot(mlp_rows, gate_full, preferred_element_type=F32)
    up_pre = jnp.dot(mlp_rows, up_full, preferred_element_type=F32)
    sigmoid_gate = jax.nn.sigmoid(gate_pre)
    activated = gate_pre * sigmoid_gate
    hidden = (activated * up_pre).astype(BF16)
    down_grad = dot(hidden, grad_rows, 0, 0).astype(BF16)
    down_out = ranks.reduce_split(down_grad, 0, 1, shard)
    grad_hidden = dot(grad_rows, down_full, 1, 1)
    grad_gate = (
        grad_hidden * up_pre * sigmoid_gate * (1.0 + gate_pre * (1.0 - sigmoid_gate))
    ).astype(BF16)
    grad_up = (grad_hidden * activated).astype(BF16)
    mlp_norm_terms = (dot(grad_gate, gate_full, 1, 1) + dot(grad_up, up_full, 1, 1)).astype(BF16)
    grad_mlp_normed = ranks.scatter_pair(mlp_norm_terms)
    gate_grad = dot(mlp_rows, grad_gate, 0, 0).astype(BF16)
    gate_out = ranks.reduce_split(gate_grad, 1, 0, shard)
    up_grad = dot(mlp_rows, grad_up, 0, 0).astype(BF16)
    up_out = ranks.reduce_split(up_grad, 1, 0, shard)
    mlp_terms = jnp.dot(hidden, down_full, preferred_element_type=F32).astype(BF16)
    result = (residual + ranks.scatter_pair(mlp_terms)).astype(BF16)

    grad_resid_norm, mlp_gain_part = rms_backward(grad_mlp_normed, mlp_normed, mlp_scale, mlp_g)
    grad_residual = grad_output.astype(F32) + grad_resid_norm
    grad_attn = ranks.gather_group(grad_residual.astype(BF16))
    grad_attended = dot(grad_attn, out_weight, 1, 1).astype(BF16)
    output_grad = dot(attended, grad_attn, 0, 0).astype(BF16)
    output_out = ranks.reduce(
        {o: ranks.block(output_grad, o, shard, 1) for o in range(n_dp)}, ranks.all_bits
    )[0]
    grad_q, grad_kv = attend_backward(
        qkv, grad_attended, inv, seg_col, seg_row, cosine, sine, n_q
    )
    grad_qkv = jnp.concatenate([grad_q, grad_kv], axis=1)
    qkv_grad = dot(attn_rows, grad_qkv, 0, 0).astype(BF16)
    qkv_out = ranks.reduce(
        {o: ranks.block(qkv_grad, o, shard, 0) for o in range(n_dp)}, ranks.all_bits
    )[0]
    attn_norm_terms = dot(grad_qkv, qkv_weight, 1, 1).astype(BF16)
    grad_attn_normed = ranks.scatter_group(attn_norm_terms)
    grad_in_norm, attn_gain_part = rms_backward(grad_attn_normed, attn_normed, attn_scale, attn_g)
    grad_input = grad_residual + grad_in_norm
    gain_sums = ranks.sum_everywhere(jnp.stack([attn_gain_part, mlp_gain_part]))
    gain_sums = ranks.block(gain_sums, 0, shard, 1)
    return (
        result,
        grad_input,
        gain_sums[0],
        unpaired_heads(qkv_out[:, :n_q], 1, repeat),
        qkv_out[:, n_q : n_q + n_kv],
        qkv_out[:, n_q + n_kv :],
        unpaired_heads(output_out, 0, repeat),
        gain_sums[1],
        gate_out,
        up_out,
        down_out,
    )


def solution(mesh):
    tokens, both, turned = P(("dp", "tensor"), None), P("dp", "tensor"), P("tensor", "dp")
    return jax.shard_map(
        functools.partial(per_device, mesh.shape["dp"], mesh.shape["tensor"]),
        mesh=mesh,
        in_specs=(
            tokens,
            P("dp"),
            P("dp"),
            both,
            both,
            both,
            turned,
            P("dp"),
            both,
            both,
            turned,
            tokens,
        ),
        out_specs=(
            tokens,
            tokens,
            P("dp"),
            both,
            both,
            both,
            turned,
            P("dp"),
            both,
            both,
            turned,
        ),
        check_vma=False,
    )
```
